32 devices in a mesh: gx: 2 (over y), gy: 4 (over x, core), gz: 4 (over z).
Axes of the slice: x: 2, y: 2, z: 4, core: 2. Of those that a mesh axis runs over, the one named last changes fastest.
Arguments:
- tokens: bfloat16 [256, 8192], P('gx', 'gy'), may hold values from -6 to 6
- cotangent: bfloat16 [256, 8192], P('gx', 'gy'), may hold values from -6 to 6
- gate_weight: bfloat16 [8192, 28672], P('gy', ('gx', 'gz')), may hold values from -5.7452426 to 5.7452426
- up_weight: bfloat16 [8192, 28672], P('gy', ('gx', 'gz')), may hold values from -5.7452426 to 5.7452426
- down_weight: bfloat16 [28672, 8192], P(('gx', 'gz'), 'gy'), may hold values from -3.0709613 to 3.0709613
- gate_reduce: bfloat16 [8192, 32], P('gy'), may hold values from -0.0625 to 0.0625
- gate_expand: bfloat16 [32, 28672], P(None, ('gx', 'gz')), may hold values from -5 to 5
- gate_magnitude: float32 [28672], P(('gx', 'gz')), may hold values from 0.5 to 2
- up_reduce: bfloat16 [8192, 32], P('gy'), may hold values from -0.0625 to 0.0625
- up_expand: bfloat16 [32, 28672], P(None, ('gx', 'gz')), may hold values from -5 to 5
- up_magnitude: float32 [28672], P(('gx', 'gz')), may hold values from 0.5 to 2
- down_reduce: bfloat16 [28672, 32], P(('gx', 'gz')), may hold values from -0.03125 to 0.03125
- down_expand: bfloat16 [32, 8192], P(None, 'gy'), may hold values from -5 to 5
- down_magnitude: float32 [8192], P('gy'), may hold values from 0.5 to 2
Outputs:
- output: bfloat16 [256, 8192], P('gx', 'gy')
- grad_tokens: bfloat16 [256, 8192], P('gx', 'gy')
- grad_gate_reduce: float32 [8192, 32], P('gy')
- grad_gate_expand: float32 [32, 28672], P(None, ('gx', 'gz'))
- grad_gate_magnitude: float32 [28672], P(('gx', 'gz'))
- grad_up_reduce: float32 [8192, 32], P('gy')
- grad_up_expand: float32 [32, 28672], P(None, ('gx', 'gz'))
- grad_up_magnitude: float32 [28672], P(('gx', 'gz'))
- grad_down_reduce: float32 [28672, 32], P(('gx', 'gz'))
- grad_down_expand: float32 [32, 8192], P(None, 'gy')
- grad_down_magnitude: float32 [8192], P('gy')
The draws below stay inside these ranges and needn't reach their ends.
All inputs are finite; a program needn't handle non-finite values.
Results may differ from the reference program's by a relative error of at most 0.012.
Values may be sent and summed in bfloat16 or wider, within the bound.
No kernel may reach another device: no remote copies, remote signals or barrier semaphores. Data moves between devices by JAX's collectives and lax.ppermute only.
A program may use at most 128 MiB of HBM per device.

```python
import math
import jax
import jax.numpy as jnp
from jax import lax

D = 8192
FF = 28672
R = 32
TOKENS = 256


def weight_law(key, in_rows, columns):
    key_base = jax.random.fold_in(key, 0)
    key_row = jax.random.fold_in(key, 2)
    key_col = jax.random.fold_in(key, 3)
    position = jnp.arange(in_rows, dtype=jnp.float32) / in_rows
    spread = 1.15
    entries = jax.random.truncated_normal(key_base, -4.0, 4.0, (in_rows, columns), jnp.float32)
    row_scale = jnp.exp(math.log(3.0) * position + jax.random.uniform(key_row, (in_rows,), jnp.float32, -spread, spread))
    col_scale = jnp.exp(jax.random.uniform(key_col, (columns,), jnp.float32, 0.0, math.log(10.0)))
    values = entries * row_scale[:, None] * col_scale[None, :] / math.sqrt(in_rows)
    return values.astype(jnp.bfloat16)


def draw_gate_weight(key, part):
    return weight_law(jax.random.fold_in(key, 11), D, FF)


def draw_up_weight(key, part):
    return weight_law(jax.random.fold_in(key, 12), D, FF)


def draw_down_weight(key, part):
    return weight_law(jax.random.fold_in(key, 13), FF, D)


def shard_levels(rng, shape, cuts, least, largest):
    factor_of, own = 1.0, jax.random.fold_in(rng, 6)
    for dim, blocks in cuts:
        heights = jnp.exp(jax.random.uniform(jax.random.fold_in(own, dim), (blocks,), jnp.float32, least / len(cuts), largest / len(cuts)))
        factor_of = factor_of * jnp.repeat(heights, shape[dim] // blocks).reshape([-1 if axis == dim else 1 for axis in range(len(shape))])
    return factor_of


def scatter_about(key, dims, width, bound, shards=(), held_as=jnp.bfloat16):
    result = width * jax.random.normal(key, dims, jnp.float32)
    if shards:
        result = result * shard_levels(key, dims, shards, -0.22, 0.18)
    return jnp.clip(result, -bound, bound).astype(held_as)


def setup_inputs(seed: int = 0) -> dict:
    streams_of = jax.random.split(jax.random.key(seed), 15)
    return {
        "tokens": scatter_about(streams_of[0], (TOKENS, D), 1.0, 6.0, ((0, 2), (1, 4))),
        "cotangent": scatter_about(streams_of[1], (TOKENS, D), 1.0, 6.0, ((0, 2), (1, 4))),
        "gate_weight": draw_gate_weight(jax.random.fold_in(streams_of[14], 71), 0),
        "up_weight": draw_up_weight(jax.random.fold_in(streams_of[14], 71), 0),
        "down_weight": draw_down_weight(jax.random.fold_in(streams_of[14], 71), 0),
        "gate_reduce": scatter_about(streams_of[5], (D, R), D ** -0.5, 0.0625, ((0, 4),)),
        "gate_expand": scatter_about(streams_of[6], (R, FF), 0.35, 5.0, ((1, 8),)),
        "gate_magnitude": jnp.clip(jnp.exp(math.log(2.0) - 1.3862944 * jax.random.uniform(streams_of[7], (FF,), jnp.float32) ** shard_levels(streams_of[7], (FF,), ((0, 8),), -0.2, 0.2)), 0.5, 2.0),
        "up_reduce": scatter_about(streams_of[8], (D, R), D ** -0.5, 0.0625, ((0, 4),)),
        "up_expand": scatter_about(streams_of[9], (R, FF), 0.35, 5.0, ((1, 8),)),
        "up_magnitude": jnp.clip(jnp.exp(math.log(2.0) - 1.3862944 * jax.random.uniform(streams_of[10], (FF,), jnp.float32) ** shard_levels(streams_of[10], (FF,), ((0, 8),), -0.2, 0.2)), 0.5, 2.0),
        "down_reduce": scatter_about(streams_of[11], (FF, R), FF ** -0.5, 0.03125, ((0, 8),)),
        "down_expand": scatter_about(streams_of[12], (R, D), 0.35, 5.0, ((1, 4),)),
        "down_magnitude": jnp.clip(jnp.exp(math.log(2.0) - 1.3862944 * jax.random.uniform(streams_of[13], (D,), jnp.float32) ** shard_levels(streams_of[13], (D,), ((0, 4),), -0.2, 0.2)), 0.5, 2.0),
    }


EPSILON = 1e-06

def column_norm(weight, reduce_in, expand_out):
    in_rows = weight.shape[0]
    blocks = 16
    weight_blocks = weight.reshape(blocks, in_rows // blocks, weight.shape[1])
    reduce_blocks = reduce_in.reshape(blocks, in_rows // blocks, reduce_in.shape[1])

    def add_block(running, pieces):
        weight_part, reduce_part = pieces
        merged = weight_part.astype(jnp.float32) + jnp.dot(reduce_part, expand_out, preferred_element_type=jnp.float32)
        return (running + lax.optimization_barrier(jnp.sum(merged * merged, axis=0)), None)
    initial = jnp.zeros((weight.shape[1],), jnp.float32)
    running, unused = lax.scan(add_block, initial, (weight_blocks, reduce_blocks))
    return jnp.sqrt(running + EPSILON)

def lowrank_linear(inputs, weight, reduce_in, expand_out):
    low_part = jnp.dot(inputs, reduce_in, preferred_element_type=jnp.float32).astype(jnp.bfloat16)
    linear = jnp.dot(inputs, weight, preferred_element_type=jnp.float32) + jnp.dot(low_part, expand_out, preferred_element_type=jnp.float32)
    return (linear, low_part)

def reference(tokens, cotangent, gate_weight, up_weight, down_weight, gate_reduce, gate_expand, gate_magnitude, up_reduce, up_expand, up_magnitude, down_reduce, down_expand, down_magnitude):
    norm_gate = column_norm(gate_weight, gate_reduce, gate_expand)
    norm_up = column_norm(up_weight, up_reduce, up_expand)
    norm_down = column_norm(down_weight, down_reduce, down_expand)
    scale_gate = gate_magnitude / norm_gate
    scale_up = up_magnitude / norm_up
    scale_down = down_magnitude / norm_down
    gate_lin, gate_low = lowrank_linear(tokens, gate_weight, gate_reduce, gate_expand)
    up_lin, up_low = lowrank_linear(tokens, up_weight, up_reduce, up_expand)
    gate_pre = gate_lin * scale_gate[None, :]
    up_pre = up_lin * scale_up[None, :]
    sigmoid_gate = jax.nn.sigmoid(gate_pre)
    active = gate_pre * sigmoid_gate
    hidden = (active * up_pre).astype(jnp.bfloat16)
    down_lin, down_low = lowrank_linear(hidden, down_weight, down_reduce, down_expand)
    output = (down_lin * scale_down[None, :]).astype(jnp.bfloat16)
    cot_float = cotangent.astype(jnp.float32)
    down_delta = (cot_float * scale_down[None, :]).astype(jnp.bfloat16)
    grad_down_magnitude = lax.optimization_barrier(jnp.sum(cot_float * down_lin, axis=0)) / norm_down
    grad_down_expand = jnp.dot(down_low.T, down_delta, preferred_element_type=jnp.float32)
    down_back = jnp.dot(down_delta, down_expand.T, preferred_element_type=jnp.float32).astype(jnp.bfloat16)
    grad_down_reduce = jnp.dot(hidden.T, down_back, preferred_element_type=jnp.float32)
    hidden_grad = (jnp.dot(down_delta, down_weight.T, preferred_element_type=jnp.float32) + jnp.dot(down_back, down_reduce.T, preferred_element_type=jnp.float32)).astype(jnp.bfloat16)
    hgrad_float = hidden_grad.astype(jnp.float32)
    gate_grad = hgrad_float * up_pre * sigmoid_gate * (1.0 + gate_pre * (1.0 - sigmoid_gate))
    up_grad = hgrad_float * active
    gate_delta = (gate_grad * scale_gate[None, :]).astype(jnp.bfloat16)
    up_delta = (up_grad * scale_up[None, :]).astype(jnp.bfloat16)
    grad_gate_magnitude = lax.optimization_barrier(jnp.sum(gate_grad * gate_lin, axis=0)) / norm_gate
    grad_up_magnitude = lax.optimization_barrier(jnp.sum(up_grad * up_lin, axis=0)) / norm_up
    grad_gate_expand = jnp.dot(gate_low.T, gate_delta, preferred_element_type=jnp.float32)
    grad_up_expand = jnp.dot(up_low.T, up_delta, preferred_element_type=jnp.float32)
    gate_back = jnp.dot(gate_delta, gate_expand.T, preferred_element_type=jnp.float32).astype(jnp.bfloat16)
    up_back = jnp.dot(up_delta, up_expand.T, preferred_element_type=jnp.float32).astype(jnp.bfloat16)
    grad_gate_reduce = jnp.dot(tokens.T, gate_back, preferred_element_type=jnp.float32)
    grad_up_reduce = jnp.dot(tokens.T, up_back, preferred_element_type=jnp.float32)
    grad_tokens = (jnp.dot(gate_delta, gate_weight.T, preferred_element_type=jnp.float32) + jnp.dot(up_delta, up_weight.T, preferred_element_type=jnp.float32) + jnp.dot(gate_back, gate_reduce.T, preferred_element_type=jnp.float32) + jnp.dot(up_back, up_reduce.T, preferred_element_type=jnp.float32)).astype(jnp.bfloat16)
    return (output, grad_tokens, grad_gate_reduce, grad_gate_expand, grad_gate_magnitude, grad_up_reduce, grad_up_expand, grad_up_magnitude, grad_down_reduce, grad_down_expand, grad_down_magnitude)
```

```python
import jax
import jax.numpy as jnp
from jax import lax
from jax.sharding import PartitionSpec as P

EPSILON = 1e-06


def tile_square(weight, reduce_in, expand_out):
    merged = weight.astype(jnp.float32) + jnp.dot(
        reduce_in, expand_out, preferred_element_type=jnp.float32
    )
    return jnp.sum(merged * merged, axis=0)


def swap(values, axis, bit):
    count = lax.axis_size(axis)
    return lax.ppermute(values, axis, [(i, i ^ bit) for i in range(count)])


def all_sum(values, *axes):
    for axis in axes:
        bit = 1
        while bit < lax.axis_size(axis):
            values = values + swap(values, axis, bit)
            bit *= 2
    return values


def own_rows(values, axis):
    rows = values.shape[0] // lax.axis_size(axis)
    return lax.dynamic_slice_in_dim(values, lax.axis_index(axis) * rows, rows, 0)


def flip(values, axis):
    count = lax.axis_size(axis)
    rows = values.shape[0] // count
    index = lax.axis_index(axis)
    return jnp.concatenate(
        [
            lax.dynamic_slice_in_dim(values, jnp.bitwise_xor(index, p) * rows, rows, 0)
            for p in range(count)
        ],
        axis=0,
    )


def scatter_sum(values, axis):
    count = lax.axis_size(axis)
    rows, columns = values.shape
    block = rows // count
    values = values.astype(jnp.bfloat16).reshape(count, block, columns)
    bit = 1
    while bit < count:
        pairs = values.reshape(values.shape[0] // 2, 2, block, columns)
        got = swap(pairs[:, 1], axis, bit)
        values = pairs[:, 0].astype(jnp.float32) + got.astype(jnp.float32)
        bit *= 2
        if bit < count:
            values = values.astype(jnp.bfloat16)
    return values.reshape(block, columns)


def gather(values, axis):
    count = lax.axis_size(axis)
    block, columns = values.shape
    values = values.reshape(1, block, columns)
    bit = count // 2
    while bit >= 1:
        got = swap(values, axis, bit)
        values = jnp.stack([values, got], axis=1).reshape(-1, block, columns)
        bit //= 2
    return flip(values.reshape(count * block, columns), axis)


def contract_last(left, right):
    return lax.dot_general(
        left, right, (((1,), (1,)), ((), ())), preferred_element_type=jnp.float32
    )


def contract_first(left, right):
    return lax.dot_general(
        left, right, (((0,), (0,)), ((), ())), preferred_element_type=jnp.float32
    )


def on_device(
    tokens,
    cotangent,
    gate_weight,
    up_weight,
    down_weight,
    gate_reduce,
    gate_expand,
    gate_magnitude,
    up_reduce,
    up_expand,
    up_magnitude,
    down_reduce,
    down_expand,
    down_magnitude,
):
    bf16 = jnp.bfloat16
    f32 = jnp.float32
    rank = gate_reduce.shape[1]
    all_tokens = gather(tokens, "gx")
    all_cot = gather(cotangent, "gx")
    square_down = tile_square(down_weight, down_reduce, down_expand)
    norm_down = jnp.sqrt(all_sum(square_down, "gx", "gz") + EPSILON)
    scale_down = down_magnitude / norm_down

    turned = flip(all_tokens, "gy")
    part_gate = jnp.dot(turned, gate_weight, preferred_element_type=f32)
    gate_sum = scatter_sum(part_gate, "gy")
    part_up = jnp.dot(turned, up_weight, preferred_element_type=f32)
    up_sum = scatter_sum(part_up, "gy")
    both_reduce = jnp.concatenate([gate_reduce, up_reduce], axis=1)
    low_sum = all_sum(jnp.dot(all_tokens, both_reduce, preferred_element_type=f32), "gy").astype(bf16)
    gate_low, up_low = low_sum[:, :rank], low_sum[:, rank:]

    square_gate = tile_square(gate_weight, gate_reduce, gate_expand)
    square_up = tile_square(up_weight, up_reduce, up_expand)
    squares = all_sum(jnp.stack([square_gate, square_up]), "gy")
    norm_gate = jnp.sqrt(squares[0] + EPSILON)
    norm_up = jnp.sqrt(squares[1] + EPSILON)
    scale_gate = gate_magnitude / norm_gate
    scale_up = up_magnitude / norm_up

    all_delta = (all_cot.astype(f32) * scale_down[None, :]).astype(bf16)
    part_hidden_grad = contract_last(flip(all_delta, "gy"), down_weight)
    hidden_gradsum = scatter_sum(part_hidden_grad, "gy")
    down_back = all_sum(contract_last(all_delta, down_expand), "gy").astype(bf16)

    low_own = own_rows(low_sum, "gy")
    gate_lin = gate_sum + jnp.dot(low_own[:, :rank], gate_expand, preferred_element_type=f32)
    up_lin = up_sum + jnp.dot(low_own[:, rank:], up_expand, preferred_element_type=f32)
    gate_pre = gate_lin * scale_gate[None, :]
    up_pre = up_lin * scale_up[None, :]
    sigmoid_gate = jax.nn.sigmoid(gate_pre)
    active = gate_pre * sigmoid_gate
    hidden = (active * up_pre).astype(bf16)
    all_hidden = gather(hidden, "gy")

    hidden_grad = (
        hidden_gradsum + contract_last(own_rows(down_back, "gy"), down_reduce)
    ).astype(bf16)
    hgrad_float = hidden_grad.astype(f32)
    gate_grad = hgrad_float * up_pre * sigmoid_gate * (1.0 + gate_pre * (1.0 - sigmoid_gate))
    up_grad = hgrad_float * active
    gate_delta = (gate_grad * scale_gate[None, :]).astype(bf16)
    up_delta = (up_grad * scale_up[None, :]).astype(bf16)
    all_gate_delta = gather(gate_delta, "gy")
    all_up_delta = gather(up_delta, "gy")
    magnitudes = all_sum(
        jnp.stack([jnp.sum(gate_grad * gate_lin, axis=0), jnp.sum(up_grad * up_lin, axis=0)]),
        "gy",
    )
    grad_gate_magnitude = magnitudes[0] / norm_gate
    grad_up_magnitude = magnitudes[1] / norm_up

    part_down = jnp.dot(all_hidden, down_weight, preferred_element_type=f32).astype(bf16)
    down_rows = scatter_sum(flip(part_down, "gx"), "gx").astype(bf16)
    down_rows = scatter_sum(flip(down_rows, "gz"), "gz")
    down_low = all_sum(
        jnp.dot(all_hidden, down_reduce, preferred_element_type=f32), "gx", "gz"
    ).astype(bf16)
    low_rows = own_rows(own_rows(down_low, "gx"), "gz")
    down_lin = down_rows + jnp.dot(low_rows, down_expand, preferred_element_type=f32)
    output = gather((down_lin * scale_down[None, :]).astype(bf16), "gz")
    cot_rows = own_rows(cotangent, "gz").astype(f32)
    grad_down_magnitude = (
        all_sum(jnp.sum(cot_rows * down_lin, axis=0), "gx", "gz") / norm_down
    )
    grad_down_expand = contract_first(down_low, all_delta)
    grad_down_reduce = contract_first(all_hidden, down_back)

    part_input = contract_last(all_gate_delta, gate_weight) + contract_last(all_up_delta, up_weight)
    input_rows = scatter_sum(flip(part_input.astype(bf16), "gx"), "gx").astype(bf16)
    input_rows = scatter_sum(flip(input_rows, "gz"), "gz")
    backs = all_sum(
        jnp.concatenate(
            [
                contract_last(all_gate_delta, gate_expand),
                contract_last(all_up_delta, up_expand),
            ],
            axis=1,
        ),
        "gx",
        "gz",
    ).astype(bf16)
    gate_back, up_back = backs[:, :rank], backs[:, rank:]
    back_rows = own_rows(own_rows(backs, "gx"), "gz")
    grad_tokens = gather(
        (input_rows + contract_last(back_rows, both_reduce)).astype(bf16), "gz"
    )
    grad_gate_expand = contract_first(gate_low, all_gate_delta)
    grad_up_expand = contract_first(up_low, all_up_delta)
    grad_gate_reduce = contract_first(all_tokens, gate_back)
    grad_up_reduce = contract_first(all_tokens, up_back)
    return (
        output,
        grad_tokens,
        grad_gate_reduce,
        grad_gate_expand,
        grad_gate_magnitude,
        grad_up_reduce,
        grad_up_expand,
        grad_up_magnitude,
        grad_down_reduce,
        grad_down_expand,
        grad_down_magnitude,
    )


def solution(mesh):
    return jax.shard_map(
        on_device,
        mesh=mesh,
        in_specs=(
            P("gx", "gy"),
            P("gx", "gy"),
            P("gy", ("gx", "gz")),
            P("gy", ("gx", "gz")),
            P(("gx", "gz"), "gy"),
            P("gy", None),
            P(None, ("gx", "gz")),
            P(("gx", "gz")),
            P("gy", None),
            P(None, ("gx", "gz")),
            P(("gx", "gz")),
            P(("gx", "gz"), None),
            P(None, "gy"),
            P("gy"),
        ),
        out_specs=(
            P("gx", "gy"),
            P("gx", "gy"),
            P("gy", None),
            P(None, ("gx", "gz")),
            P(("gx", "gz")),
            P("gy", None),
            P(None, ("gx", "gz")),
            P(("gx", "gz")),
            P(("gx", "gz"), None),
            P(None, "gy"),
            P("gy"),
        ),
        check_vma=False,
    )
```
